32 devices in a mesh: groups: 2 (over y), hidden: 4 (over z), width: 2 (over x), rep: 2 (over core).
Axes of the slice: x: 2, y: 2, z: 4, core: 2. Of those that a mesh axis runs over, the one named last changes fastest.
Arguments:
- tokens: bfloat16 [1024, 5120], P(('groups', 'rep'), 'width'), parts along dimension 0, may hold values from -6 to 6
- w_gate: bfloat16 [5120, 13824], P(('width', 'rep'), 'hidden'), may hold values from -0.078125 to 0.078125
- w_up: bfloat16 [5120, 13824], P(('width', 'rep'), 'hidden'), may hold values from -0.078125 to 0.078125
- w_down: bfloat16 [13824, 5120], P('hidden', ('width', 'rep')), may hold values from -0.0546875 to 0.0546875
- keep_a: int32 [128], P('hidden'), may hold values from 0 to 1, as said below
- keep_b: int32 [128], P('hidden'), may hold values from 0 to 1, as said below
Outputs:
- grad_gate_a: bfloat16 [5120, 20736], P(('width', 'rep'), ('groups', 'hidden')), parts along dimension 1
- grad_up_a: bfloat16 [5120, 20736], P(('width', 'rep'), ('groups', 'hidden')), parts along dimension 1
- grad_down_a: bfloat16 [20736, 5120], P(('groups', 'hidden'), ('width', 'rep')), parts along dimension 0
- grad_gate_b: bfloat16 [5120, 13824], P(('width', 'rep'), ('groups', 'hidden')), parts along dimension 1
- grad_up_b: bfloat16 [5120, 13824], P(('width', 'rep'), ('groups', 'hidden')), parts along dimension 1
- grad_down_b: bfloat16 [13824, 5120], P(('groups', 'hidden'), ('width', 'rep')), parts along dimension 0
- losses: float32 [4], P('groups'), parts along dimension 0
The draws below stay inside these ranges and needn't reach their ends.
There are 2 independent parts, one for each index of `groups`. The reference program is written for one: setup_inputs(seed, part) draws one part's arguments, and reference() takes and returns one part's arrays. A program takes and returns all parts, laid end to end along the dimension named above; an argument that names none is the same for every part. Nothing has to cross between parts.
Inputs may be any that keep to these rules, and one draw needn't show every extreme that they name: `keep_a`: 0 or 1 for each block of 108 units of the parent; 6912 units are kept in all; each shard of 32 consecutive blocks keeps at most 24, and some shard keeps exactly 24. `keep_b`: 0 or 1 for each block of 108 units of the parent; 3456 units are kept in all; each shard of 32 consecutive blocks keeps at most 16, and some shard keeps exactly 16.
All inputs are finite; a program needn't handle non-finite values.
Results may differ from the reference program's by a relative error of at most 0.0075.
Values may be sent and summed in bfloat16 or wider, within the bound.
A program may use at most 192 MiB of HBM per device.

```python
import jax
import jax.numpy as jnp

D = 5120
FF = 13824
BLOCK = 108
TOKENS = 512
SHARD_BLOCKS = 32
SLOT_A = 24
SLOT_B = 16


def keep_table(key, middle, spread, salt_value):
    shards = FF // BLOCK // SHARD_BLOCKS
    shard_order = jax.random.permutation(jax.random.fold_in(key, salt_value), shards)
    heavy_shards = (shard_order < shards // 2).astype(jnp.int32)
    counts = middle - spread + 2 * spread * heavy_shards
    scores = jax.random.randint(jax.random.fold_in(key, salt_value + 1), (shards, SHARD_BLOCKS), 0, 1 << 20) * SHARD_BLOCKS
    scores = scores + jnp.arange(SHARD_BLOCKS, dtype=jnp.int32)[None, :]
    ranking = jnp.argsort(jnp.argsort(scores, axis=1), axis=1)
    return (ranking < counts[:, None]).astype(jnp.int32).reshape(-1)


def draw_keep_a(key, part):
    return keep_table(key, SHARD_BLOCKS // 2, SHARD_BLOCKS // 4, 101)


def draw_keep_b(key, part):
    return keep_table(key, SHARD_BLOCKS // 4, SHARD_BLOCKS // 4, 203)


def block_scale(stream_key, dims, cuts, smallest, top_value):
    gain = 1.0
    for dim, blocks in cuts:
        draws = jax.random.uniform(jax.random.fold_in(jax.random.fold_in(stream_key, 6), dim), (blocks,), jnp.float32, smallest / len(cuts), top_value / len(cuts))
        gain = gain * jnp.repeat(jnp.exp(draws), dims[dim] // blocks).reshape((-1,) + (1,) * (len(dims) - 1 - dim))
    return gain


def noise(rng, shape, scale, reach, split=(), kind=jnp.bfloat16):
    entries = jax.random.normal(rng, shape, jnp.float32) * scale
    if len(split) > 0:
        entries = block_scale(rng, shape, split, -0.22, 0.18) * entries
    return jnp.clip(entries, min=-reach, max=reach).astype(kind)


def setup_inputs(seed: int = 0, part: int = 0) -> dict:
    key_list = jax.random.split(jax.random.key(seed), 7)
    own_keys = jax.random.split(jax.random.fold_in(key_list[6], part), 7)
    tokens = noise(own_keys[0], (TOKENS, D), 1.0, 6.0, ((0, 2), (1, 2)))
    w_gate = noise(key_list[1], (D, FF), D ** -0.5, 0.078125, ((0, 4), (1, 4)))
    w_up = noise(key_list[2], (D, FF), D ** -0.5, 0.078125, ((0, 4), (1, 4)))
    w_down = noise(key_list[3], (FF, D), FF ** -0.5, 0.0546875, ((0, 4), (1, 4)))
    keep_a = draw_keep_a(jax.random.fold_in(key_list[6], 71), part)
    keep_b = draw_keep_b(jax.random.fold_in(key_list[6], 71), part)
    return dict(tokens=tokens, w_gate=w_gate, w_up=w_up, w_down=w_down, keep_a=keep_a, keep_b=keep_b)


def slot_columns(keep_mask, slot_count):
    groups = keep_mask.reshape(-1, SHARD_BLOCKS)
    ranking = (jnp.cumsum(groups, axis=1) - 1).astype(jnp.int32)
    slot_ids = jnp.arange(slot_count, dtype=jnp.int32)
    matches = groups[:, None, :] * (ranking[:, None, :] == slot_ids[None, :, None]).astype(jnp.int32)
    positions = jnp.arange(SHARD_BLOCKS, dtype=jnp.int32)
    offsets = (jnp.arange(groups.shape[0], dtype=jnp.int32) * SHARD_BLOCKS)[:, None]
    block_index = (jnp.sum(matches * positions[None, None, :], axis=2) + offsets).astype(jnp.int32)
    block_live = jnp.sum(matches, axis=2).astype(jnp.int32)
    columns = (block_index[:, :, None] * BLOCK + jnp.arange(BLOCK, dtype=jnp.int32)[None, None, :]).reshape(-1).astype(jnp.int32)
    live = jnp.broadcast_to(block_live[:, :, None], block_live.shape + (BLOCK,)).reshape(-1)
    return columns, live


def reference(tokens, w_gate, w_up, w_down, keep_a, keep_b):
    gate_value = jnp.dot(tokens, w_gate, preferred_element_type=jnp.float32)
    up_value = jnp.dot(tokens, w_up, preferred_element_type=jnp.float32)
    sigmoid_term = jax.nn.sigmoid(gate_value)
    activation = jax.nn.silu(gate_value)
    slope_term = sigmoid_term * (1.0 + gate_value * (1.0 - sigmoid_term))
    hidden = (activation * up_value).astype(jnp.bfloat16)
    outputs = []
    loss_list = []
    for keep_mask, slot_count in ((keep_a, SLOT_A), (keep_b, SLOT_B)):
        dropped = (1 - jnp.repeat(keep_mask, BLOCK)).astype(jnp.bfloat16)
        difference = -jnp.dot(hidden * dropped[None, :], w_down, preferred_element_type=jnp.float32)
        loss_list.append(jnp.sum(difference * difference) / (TOKENS * D))
        errors = difference.astype(jnp.bfloat16)
        columns, live = slot_columns(keep_mask, slot_count)
        live_float = live.astype(jnp.float32)
        hidden_slot = jnp.take(hidden, columns, axis=1) * live.astype(jnp.bfloat16)[None, :]
        grad_down = jnp.dot(hidden_slot.T, errors, preferred_element_type=jnp.float32).astype(jnp.bfloat16)
        back_total = jnp.dot(errors, jnp.take(w_down, columns, axis=0).T, preferred_element_type=jnp.float32)
        delta_gate = (back_total * jnp.take(up_value, columns, axis=1) * jnp.take(slope_term, columns, axis=1) * live_float[None, :]).astype(jnp.bfloat16)
        delta_up = (back_total * jnp.take(activation, columns, axis=1) * live_float[None, :]).astype(jnp.bfloat16)
        grad_gate = jnp.dot(tokens.T, delta_gate, preferred_element_type=jnp.float32).astype(jnp.bfloat16)
        grad_up = jnp.dot(tokens.T, delta_up, preferred_element_type=jnp.float32).astype(jnp.bfloat16)
        outputs.append((grad_gate, grad_up, grad_down))
    losses = jnp.stack(loss_list).astype(jnp.float32)
    return (outputs[0][0], outputs[0][1], outputs[0][2], outputs[1][0], outputs[1][1], outputs[1][2], losses)
```

```python
import functools

import jax
import jax.numpy as jnp
from jax import lax
from jax.experimental import pallas as pl
from jax.experimental.pallas import tpu as pltpu
from jax.sharding import PartitionSpec as P


D = 5120
BLOCK = 108


def block_slots(keep_mask, slot_count):
    positions = jnp.arange(keep_mask.shape[0], dtype=jnp.int32)
    ranking = jnp.cumsum(keep_mask) - 1
    slot_ids = jnp.arange(slot_count, dtype=jnp.int32)
    matches = keep_mask[None, :] * (ranking[None, :] == slot_ids[:, None]).astype(jnp.int32)
    block_index = jnp.sum(matches * positions[None, :], axis=1)
    block_live = jnp.sum(matches, axis=1)
    return (block_index, block_live)


def pick_blocks(matrix, block_index, block_live, dim_axis):
    if dim_axis == 1:
        grouped = matrix.reshape(matrix.shape[0], -1, BLOCK)
        picked = jnp.take(grouped, block_index, axis=1) * block_live[None, :, None].astype(
            matrix.dtype
        )
        return picked.reshape(matrix.shape[0], -1)
    grouped = matrix.reshape(-1, BLOCK, matrix.shape[1])
    picked = jnp.take(grouped, block_index, axis=0) * block_live[:, None, None].astype(matrix.dtype)
    return picked.reshape(-1, matrix.shape[1])


def per_device(tokens, w_gate, w_up, w_down, keep_a, keep_b):
    gathered = lax.all_to_all(tokens, "rep", split_axis=1, concat_axis=0, tiled=True)
    part_gate = jnp.dot(gathered, w_gate, preferred_element_type=jnp.float32)
    part_up = jnp.dot(gathered, w_up, preferred_element_type=jnp.float32)
    gate_value, up_value = lax.psum((part_gate, part_up), ("width", "rep"))
    sigmoid_term = jax.nn.sigmoid(gate_value)
    activation = gate_value * sigmoid_term
    slope_term = sigmoid_term * (1.0 + gate_value * (1.0 - sigmoid_term))
    hidden = (activation * up_value).astype(jnp.bfloat16)
    shard_blocks = keep_a.shape[0]
    variant_plans = ((keep_a, 3 * shard_blocks // 4), (keep_b, shard_blocks // 2))
    differences = jnp.stack(
        [
            -jnp.dot(
                hidden * (1 - jnp.repeat(keep_mask, BLOCK)).astype(jnp.bfloat16)[None, :],
                w_down,
                preferred_element_type=jnp.float32,
            )
            for keep_mask, slot_count in variant_plans
        ]
    )
    scale_count = gathered.shape[0] * D
    totals = lax.psum(differences, "hidden")
    squares = jnp.sum(totals * totals, axis=(1, 2))
    losses = lax.psum(squares, ("width", "rep")) / scale_count
    errors = totals.astype(jnp.bfloat16)
    slot_plans = [block_slots(keep_mask, slot_count) for keep_mask, slot_count in variant_plans]
    back_terms = [
        jnp.einsum(
            "td,fd->tf",
            errors[variant],
            pick_blocks(w_down, slot_plans[variant][0], slot_plans[variant][1], 0),
            preferred_element_type=jnp.float32,
        )
        for variant in range(2)
    ]
    back_a, back_b = lax.psum((back_terms[0], back_terms[1]), ("width", "rep"))
    results = []
    for variant, back_total in ((0, back_a), (1, back_b)):
        block_index, block_live = slot_plans[variant]
        keep_mask = variant_plans[variant][0]
        up_slot = pick_blocks(up_value, block_index, block_live, 1)
        slope_slot = pick_blocks(slope_term, block_index, block_live, 1)
        act_slot = pick_blocks(activation, block_index, block_live, 1)
        hidden_slot = pick_blocks(hidden, block_index, block_live, 1)
        delta_gate = (back_total * up_slot * slope_slot).astype(jnp.bfloat16)
        delta_up = (back_total * act_slot).astype(jnp.bfloat16)
        grad_gate = jnp.einsum(
            "td,tf->df", gathered, delta_gate, preferred_element_type=jnp.float32
        )
        grad_up = jnp.einsum("td,tf->df", gathered, delta_up, preferred_element_type=jnp.float32)
        grad_down = jnp.einsum(
            "tf,td->fd", hidden_slot, errors[variant], preferred_element_type=jnp.float32
        )
        results.append(
            (
                grad_gate.astype(jnp.bfloat16),
                grad_up.astype(jnp.bfloat16),
                grad_down.astype(jnp.bfloat16),
            )
        )
    return (
        results[0][0],
        results[0][1],
        results[0][2],
        results[1][0],
        results[1][1],
        results[1][2],
        losses,
    )


LANES = 128
TILE = 256
WINDOWS = (TILE - 2) // BLOCK + 2
SWAP = [(0, 1), (1, 0)]


def lane_kernel(slots, start_ref, live_ref, x_ref, o_ref):
    base = pl.program_id(0) * TILE
    first = base // BLOCK
    last = x_ref.shape[1] // LANES - 2
    rows = lax.broadcasted_iota(jnp.int32, (2 * LANES, TILE), 0)
    columns = lax.broadcasted_iota(jnp.int32, (2 * LANES, TILE), 1)
    total = jnp.zeros(o_ref.shape, jnp.float32)
    for k in range(WINDOWS):
        slot = first + k
        known = jnp.minimum(slot, slots - 1)
        start = start_ref[known]
        limit = jnp.where(slot < slots, live_ref[known] * BLOCK, 0)
        corner = pl.multiple_of(jnp.minimum(start // LANES, last) * LANES, LANES)
        target = columns + (base - slot * BLOCK)
        match = (rows + (corner - start) == target) & (target >= 0) & (target < limit)
        pick = jnp.where(match, 1.0, 0.0).astype(jnp.bfloat16)
        total += jnp.dot(x_ref[:, pl.ds(corner, 2 * LANES)], pick, preferred_element_type=jnp.float32)
    o_ref[...] = total.astype(o_ref.dtype)


def row_kernel(slots, start_ref, live_ref, x_ref, o_ref):
    base = pl.program_id(0) * TILE
    first = base // BLOCK
    last = (x_ref.shape[0] - LANES) // 16
    rows = lax.broadcasted_iota(jnp.int32, (TILE, LANES), 0)
    columns = lax.broadcasted_iota(jnp.int32, (TILE, LANES), 1)
    picks, windows = [], []
    for k in range(WINDOWS):
        slot = first + k
        known = jnp.minimum(slot, slots - 1)
        start = start_ref[known]
        limit = jnp.where(slot < slots, live_ref[known] * BLOCK, 0)
        corner = pl.multiple_of(jnp.minimum(start // 16, last) * 16, 16)
        target = rows + (base - slot * BLOCK)
        match = (columns + (corner - start) == target) & (target >= 0) & (target < limit)
        picks.append(jnp.where(match, 1.0, 0.0).astype(jnp.bfloat16))
        windows.append(x_ref[pl.ds(corner, LANES), :])
    o_ref[...] = jnp.dot(
        jnp.concatenate(picks, axis=1),
        jnp.concatenate(windows, axis=0),
        preferred_element_type=jnp.float32,
    ).astype(o_ref.dtype)


def select_blocks(matrix, plan, axis):
    block_index, block_live = plan
    slots = block_index.shape[0]
    size = slots * BLOCK
    tiles = pl.cdiv(size, TILE)
    other = matrix.shape[1 - axis]
    if axis == 1:
        body, shape, tile = lane_kernel, (other, size), (other, TILE)
        place = lambda t, *_: (0, t)
        depth = 2 * LANES * WINDOWS
    else:
        body, shape, tile = row_kernel, (size, other), (TILE, other)
        place = lambda t, *_: (t, 0)
        depth = LANES * WINDOWS
    return pl.pallas_call(
        functools.partial(body, slots),
        out_shape=jax.ShapeDtypeStruct(shape, matrix.dtype),
        grid_spec=pltpu.PrefetchScalarGridSpec(
            num_scalar_prefetch=2,
            grid=(tiles,),
            in_specs=[pl.BlockSpec(matrix.shape, lambda t, *_: (0, 0))],
            out_specs=pl.BlockSpec(tile, place),
        ),
        compiler_params=pltpu.CompilerParams(vmem_limit_bytes=48 << 20),
        cost_estimate=pl.CostEstimate(
            flops=2 * tiles * TILE * depth * other,
            bytes_accessed=2 * (matrix.size + size * other),
            transcendentals=0,
        ),
    )(block_index * BLOCK, block_live, matrix)


def line_reduce(part, axis, count):
    me = lax.axis_index(axis)
    rows = part.shape[0] // count

    def chunk(c):
        return lax.dynamic_slice_in_dim(part, jnp.clip(c, 0, count - 1) * rows, rows, 0)

    total = chunk(me)
    for way in (1, -1):
        came = None
        for step in range(1, count):
            c = me + way * (count - step)
            sent = chunk(c)
            if came is not None:
                sent = sent + came.astype(jnp.float32)
            if way == 1:
                pairs = [(i, i + 1) for i in range(min(step, count - 1))]
            else:
                pairs = [(count - 1 - i, count - 2 - i) for i in range(min(step, count - 1))]
            came = lax.ppermute(sent.astype(jnp.bfloat16), axis, pairs)
        total = total + came.astype(jnp.float32)
    return total


def line_gather(chunk, axis, count):
    me = lax.axis_index(axis)
    rows = chunk.shape[0]
    came = {}
    for way in (1, -1):
        held = chunk
        for step in range(1, count):
            if way == 1:
                pairs = [(i, i + 1) for i in range(step - 1, count - 1)]
            else:
                pairs = [(count - 1 - i, count - 2 - i) for i in range(step - 1, count - 1)]
            held = lax.ppermute(held, axis, pairs)
            came[way, step] = held
    whole = jnp.zeros((rows * count, chunk.shape[1]), chunk.dtype)
    whole = lax.dynamic_update_slice_in_dim(whole, chunk, me * rows, 0)
    for step in range(1, count):
        piece = came[1, step] + came[-1, count - step]
        whole = lax.dynamic_update_slice_in_dim(
            whole, piece, lax.rem(me - step + count, count) * rows, 0
        )
    return whole


def swap(value, axis):
    return lax.ppermute(value, axis, SWAP)


def scatter_sum(mine, theirs):
    half = mine + swap(theirs.astype(jnp.bfloat16), "rep").astype(jnp.float32)
    rows = half.shape[0] // 2
    return half[:rows] + swap(half[rows:].astype(jnp.bfloat16), "width").astype(jnp.float32)


def gather_rows(own):
    chip = jnp.concatenate([own, swap(own, "width")], axis=0)
    return jnp.concatenate([chip, swap(chip, "rep")], axis=0)


def per_device_fast(hidden_size, tokens, w_gate, w_up, w_down, keep_a, keep_b):
    wide, core = lax.axis_index("width"), lax.axis_index("rep")
    quarter = tokens.shape[0] // 2
    depth = w_gate.shape[0]
    turned = jnp.concatenate([tokens[quarter:], tokens[:quarter]], axis=0)
    tokens = jnp.where(wide == 0, tokens, turned)
    given = lax.dynamic_slice_in_dim(tokens, (1 - core) * depth, depth, 1)
    theirs = swap(given, "rep")
    mine = lax.dynamic_slice_in_dim(tokens, core * depth, depth, 1)

    def dot(a, b, dims):
        return lax.dot_general(a, b, (dims, ((), ())), preferred_element_type=jnp.float32)

    inner = ((1,), (0,))
    shard_blocks = keep_a.shape[0]
    plans = (
        block_slots(keep_a, 3 * shard_blocks // 4),
        block_slots(keep_b, shard_blocks // 2),
    )
    gate_theirs, up_theirs = dot(theirs, w_gate, inner), dot(theirs, w_up, inner)
    gate_value = scatter_sum(dot(mine, w_gate, inner), gate_theirs)
    up_value = scatter_sum(dot(mine, w_up, inner), up_theirs)
    sigmoid_term = jax.nn.sigmoid(gate_value)
    activation = gate_value * sigmoid_term
    slope_term = sigmoid_term * (1.0 + gate_value * (1.0 - sigmoid_term))
    hidden_own = (activation * up_value).astype(jnp.bfloat16)
    factors = jnp.concatenate(
        [(up_value * slope_term).astype(jnp.bfloat16), activation.astype(jnp.bfloat16)], axis=0
    )
    hidden = gather_rows(hidden_own)
    token_count = hidden.shape[0]

    every_token = jnp.concatenate([mine, theirs], axis=0)
    errors, squares = [], []
    for keep_mask in (keep_a, keep_b):
        dropped = (1 - jnp.repeat(keep_mask, BLOCK)).astype(jnp.bfloat16)
        difference = -dot(hidden * dropped[None, :], w_down, inner)
        total = line_reduce(difference, "hidden", hidden_size)
        squares.append(jnp.sum(total * total))
        errors.append(line_gather(total.astype(jnp.bfloat16), "hidden", hidden_size))
    losses = lax.psum(jnp.stack(squares), ("hidden", "width", "rep")) / (token_count * D)

    results = []
    for plan, error in zip(plans, errors):
        weight_slot = select_blocks(w_down, plan, 0)
        back = dot(error, weight_slot, ((1,), (1,)))
        half = token_count // 2
        back_own = scatter_sum(back[:half], back[half:])
        factor_slot = select_blocks(factors, plan, 1).astype(jnp.float32)
        hidden_slot = select_blocks(hidden, plan, 1)
        delta_gate = gather_rows((back_own * factor_slot[:quarter]).astype(jnp.bfloat16))
        delta_up = gather_rows((back_own * factor_slot[quarter:]).astype(jnp.bfloat16))
        outer = ((0,), (0,))
        results += [
            dot(every_token, delta_gate, outer).astype(jnp.bfloat16),
            dot(every_token, delta_up, outer).astype(jnp.bfloat16),
            dot(hidden_slot, error, outer).astype(jnp.bfloat16),
        ]
    return (*results, losses)


def solution(mesh):
    in_specs = (
        P(("groups", "rep"), "width"),
        P(("width", "rep"), "hidden"),
        P(("width", "rep"), "hidden"),
        P("hidden", ("width", "rep")),
        P("hidden"),
        P("hidden"),
    )
    out_specs = (
        P(("width", "rep"), ("groups", "hidden")),
        P(("width", "rep"), ("groups", "hidden")),
        P(("groups", "hidden"), ("width", "rep")),
        P(("width", "rep"), ("groups", "hidden")),
        P(("width", "rep"), ("groups", "hidden")),
        P(("groups", "hidden"), ("width", "rep")),
        P("groups"),
    )
    sizes = mesh.shape
    body = per_device
    if sizes["width"] == 2 and sizes["rep"] == 2 and sizes["hidden"] <= 4:
        body = functools.partial(per_device_fast, sizes["hidden"])
    return jax.shard_map(
        body, mesh=mesh, in_specs=in_specs, out_specs=out_specs, check_vma=False
    )
```
